32 devices in a mesh: mem: 8 (over z, core), slab: 4 (over y, x).
Axes of the slice: x: 2, y: 2, z: 4, core: 2. Of those that a mesh axis runs over, the one named last changes fastest.
Arguments:
- thickness: float32 [64, 256, 384], P('mem', 'slab'), may hold values from 0.5 to 2.5
- face_u: float32 [256, 384], P('slab'), may hold values from -0.4 to 0.4
- face_v: float32 [256, 384], P('slab'), may hold values from -0.4 to 0.4
- obs_cells: int32 [512, 4], P('slab'), may hold values from 0 to 98303, as said below
- obs_weights: int32 [512, 4], P('slab'), may hold values from 1 to 4
- obs_values: float32 [512], P('slab'), may hold values from -6 to 6
- obs_noise: float32 [64, 512], P('mem', 'slab'), may hold values from -3 to 3
- cov_inverse: float32 [512, 512], P('slab'), may hold values from -0.375 to 0.375
- taper_mask: int32 [4, 4], replicated, may hold values from 0 to 1, as said below
Outputs:
- analysis: float32 [64, 256, 384], P('mem', 'slab')
The draws below stay inside these ranges and needn't reach their ends.
Inputs may be any that keep to these rules, and one draw needn't show every extreme that they name: `obs_cells`: observation o covers a 2 x 2 square of cells, all within the rows of slab o // 128. `taper_mask`: entries are 0 or 1 and the diagonal is 1.
All inputs are finite; a program needn't handle non-finite values.
Results may differ from the reference program's by a relative error of at most 0.0003.
Values sent between devices are 32-bit elements; how exact they have to be, the bound alone decides.
A program may use at most 64 MiB of HBM per device.

```python
import jax
import jax.numpy as jnp
from jax import lax

ROWS_SLAB = 64
CELLS_PER_ROW = 384
OBS_SLAB = 128
FOOT = 4
ENSEMBLE_SIZE = 64
GRID_ROWS = 256
OBS = 512
N_SLAB = 4


def draw_obs_cells(key, part):
    key_row, key_col = jax.random.split(jax.random.fold_in(key, 11))
    block_of = jnp.arange(OBS, dtype=jnp.int32) // OBS_SLAB
    row_base = block_of * ROWS_SLAB + jax.random.randint(key_row, (OBS,), 0, ROWS_SLAB - 1)
    col_base = jax.random.randint(key_col, (OBS,), 0, CELLS_PER_ROW - 1)
    row_offset = jnp.array([0, 0, 1, 1], dtype=jnp.int32)
    col_offset = jnp.array([0, 1, 0, 1], dtype=jnp.int32)
    cells_flat = (row_base[:, None] + row_offset[None, :]) * CELLS_PER_ROW + col_base[:, None] + col_offset[None, :]
    return cells_flat.astype(jnp.int32)


def draw_taper_mask(key, part):
    coin_flips = jax.random.randint(jax.random.fold_in(key, 23), (N_SLAB, N_SLAB), 0, 2)
    diagonal = jnp.eye(N_SLAB, dtype=jnp.int32)
    return jnp.maximum(coin_flips, diagonal).astype(jnp.int32)


def with_ends(values, rng, smallest, high):
    index_at = [jax.random.randint(jax.random.fold_in(rng, axis), (), 0, length) for axis, length in enumerate(values.shape)]
    widest = values.shape.index(max(values.shape))
    next_to = index_at[:widest] + [(index_at[widest] + 1) % values.shape[widest]] + index_at[widest + 1:]
    return values.at[tuple(index_at)].set(smallest).at[tuple(next_to)].set(high)


def with_spikes(result, stream_key, source, target, shards_of, factor):
    owner, partner = [(jnp.arange(result.shape[axis_at]) // (result.shape[axis_at] // shards_of)).reshape([-1 if axis == axis_at else 1 for axis in range(result.ndim)]) for axis_at in (source, target)]
    chosen = jax.random.permutation(stream_key, shards_of)[partner]
    strong = (owner == chosen) | (owner == (partner + shards_of // 2) % shards_of)
    return jnp.where(strong, factor * result, result)


def shard_levels(stream_key, dims, shards, low, high):
    level, own = 1.0, jax.random.fold_in(stream_key, 6)
    for dim, blocks in shards:
        steps = jnp.exp(jax.random.uniform(jax.random.fold_in(own, dim), (blocks,), jnp.float32, low / len(shards), high / len(shards)))
        level = level * jnp.repeat(steps, dims[dim] // blocks).reshape([-1 if axis == dim else 1 for axis in range(len(dims))])
    return level


def scatter_about(key, extent, width, most, cuts=(), kind=jnp.bfloat16):
    entries = width * jax.random.normal(key, extent, jnp.float32)
    if cuts:
        entries = entries * shard_levels(key, extent, cuts, -0.22, 0.18)
    return jnp.clip(entries, -most, most).astype(kind)


def heavy_noise(rng, extent, scale, bound, pieces, heavy, kind=jnp.bfloat16):
    entries = scale * jax.random.normal(rng, extent, jnp.float32)
    if pieces:
        entries = entries * shard_levels(rng, extent, pieces, -0.22, 0.18)
    return jnp.clip(with_spikes(entries, jax.random.fold_in(rng, 3), *heavy), -bound, bound).astype(kind)


def setup_inputs(seed: int = 0) -> dict:
    streams_of = jax.random.split(jax.random.key(seed), 10)
    return {
        "thickness": jnp.clip(0.5 + 2.0 * jax.random.uniform(streams_of[0], (ENSEMBLE_SIZE, GRID_ROWS, CELLS_PER_ROW), jnp.float32) ** shard_levels(streams_of[0], (ENSEMBLE_SIZE, GRID_ROWS, CELLS_PER_ROW), ((0, 8), (1, 4)), -0.2, 0.2), 0.5, 2.5),
        "face_u": jnp.clip(jax.random.uniform(streams_of[1], (GRID_ROWS, CELLS_PER_ROW), jnp.float32, -0.4, 0.4) * shard_levels(streams_of[1], (GRID_ROWS, CELLS_PER_ROW), ((0, 4),), -0.4, 0.0), -0.4, 0.4),
        "face_v": jnp.clip(jax.random.uniform(streams_of[2], (GRID_ROWS, CELLS_PER_ROW), jnp.float32, -0.4, 0.4) * shard_levels(streams_of[2], (GRID_ROWS, CELLS_PER_ROW), ((0, 4),), -0.4, 0.0), -0.4, 0.4),
        "obs_cells": draw_obs_cells(jax.random.fold_in(streams_of[9], 71), 0),
        "obs_weights": with_ends(jax.random.randint(streams_of[4], (OBS, FOOT), 1, 5), jax.random.fold_in(streams_of[4], 1), 1, 4).astype(jnp.int32),
        "obs_values": scatter_about(streams_of[5], (OBS,), 1.0, 6.0, ((0, 4),), jnp.float32),
        "obs_noise": scatter_about(streams_of[6], (ENSEMBLE_SIZE, OBS), 0.5, 3.0, ((0, 8), (1, 4)), jnp.float32),
        "cov_inverse": heavy_noise(streams_of[7], (OBS, OBS), OBS ** -0.5, 0.375, ((0, 4),), (0, 1, 4, 2.0), jnp.float32),
        "taper_mask": draw_taper_mask(jax.random.fold_in(streams_of[9], 71), 0),
    }


def minmod(first_diff, second_diff):
    return 0.5 * (jnp.sign(first_diff) + jnp.sign(second_diff)) * jnp.minimum(jnp.abs(first_diff), jnp.abs(second_diff))


def face_flux(padded, velocity, axis_dim):
    counted = padded.shape[axis_dim] - 3
    far_low = lax.slice_in_dim(padded, 0, counted, axis=axis_dim)
    near_low = lax.slice_in_dim(padded, 1, 1 + counted, axis=axis_dim)
    near_high = lax.slice_in_dim(padded, 2, 2 + counted, axis=axis_dim)
    far_high = lax.slice_in_dim(padded, 3, 3 + counted, axis=axis_dim)
    left_state = near_low + 0.5 * minmod(near_low - far_low, near_high - near_low)
    right_state = near_high - 0.5 * minmod(near_high - near_low, far_high - near_high)
    return jnp.maximum(velocity, 0.0) * left_state + jnp.minimum(velocity, 0.0) * right_state


def reference(thickness, face_u, face_v, obs_cells, obs_weights, obs_values, obs_noise, cov_inverse, taper_mask):
    ftype = thickness.dtype
    row_pad = jnp.pad(thickness, ((0, 0), (2, 2), (0, 0)))
    row_speed = jnp.concatenate([face_v, jnp.zeros((1, CELLS_PER_ROW), ftype)], 0)
    row_fluxes = face_flux(row_pad, row_speed, 1)
    col_pad = jnp.pad(thickness, ((0, 0), (0, 0), (2, 2)))
    col_speed = jnp.concatenate([face_u, jnp.zeros((GRID_ROWS, 1), ftype)], 1)
    column_fluxes = face_flux(col_pad, col_speed, 2)
    prior_state = thickness - (column_fluxes[:, :, 1:] - column_fluxes[:, :, :-1]) - (row_fluxes[:, 1:, :] - row_fluxes[:, :-1, :])
    state_vector = prior_state.reshape(ENSEMBLE_SIZE, GRID_ROWS * CELLS_PER_ROW)
    weights = obs_weights.astype(ftype)
    picked = state_vector[:, obs_cells]
    obs_model = jnp.sum(picked * weights[None], -1) / jnp.sum(weights, -1)[None]
    innovation = obs_values[None, :] + obs_noise - obs_model
    whitened = jnp.dot(innovation, cov_inverse, precision=lax.Precision.HIGHEST)
    obs_anomaly = obs_model - jnp.mean(obs_model, 0, keepdims=True)
    anomaly = state_vector - jnp.mean(state_vector, 0, keepdims=True)
    anom_blocks = obs_anomaly.reshape(ENSEMBLE_SIZE, N_SLAB, OBS_SLAB)
    white_blocks = whitened.reshape(ENSEMBLE_SIZE, N_SLAB, OBS_SLAB)
    block_products = jnp.einsum("mbo,nbo->bmn", anom_blocks, white_blocks, precision=lax.Precision.HIGHEST)
    ensemble = jnp.einsum("sb,bmn->smn", taper_mask.astype(ftype), block_products, precision=lax.Precision.HIGHEST)
    anom_slabs = anomaly.reshape(ENSEMBLE_SIZE, N_SLAB, ROWS_SLAB * CELLS_PER_ROW)
    update = jnp.einsum("smn,msc->nsc", ensemble, anom_slabs, precision=lax.Precision.HIGHEST) / (ENSEMBLE_SIZE - 1)
    analysis = state_vector + update.reshape(ENSEMBLE_SIZE, GRID_ROWS * CELLS_PER_ROW)
    return analysis.reshape(ENSEMBLE_SIZE, GRID_ROWS, CELLS_PER_ROW)
```

```python
import functools

import jax
import jax.numpy as jnp
from jax import lax
from jax.experimental import pallas as pl
from jax.experimental.pallas import tpu as pltpu
from jax.sharding import PartitionSpec as P

MESH = pl.DeviceIdType.MESH
F32 = jnp.float32
BF16 = jnp.bfloat16


def minmod(a, b):
    return jnp.maximum(jnp.minimum(a, b), 0.0) + jnp.minimum(jnp.maximum(a, b), 0.0)


def split_blocks(rows, cols, n_mem):
    for nc in range(1, n_mem + 1):
        if n_mem % nc == 0 and cols % (128 * nc) == 0 and rows % (n_mem // nc) == 0:
            return nc, rows // (n_mem // nc)
    raise ValueError("no split")


def kernel(
    n_mem, n_slab, nc, rc,
    x_ref, u_ref, v_ref, cells_ref, wts_ref, vals_ref, noise_ref, cinv_ref, taper_ref,
    res_ref,
    t_buf, v_buf, up_buf, dn_buf, hi_rx, lo_rx, fblk, gath, outb, s_buf, rw_buf,
    om_all, p_buf, p_rx, b_buf, x_all,
    halo_s, halo_r, f_s, f_r, o_s, o_r, p_s, p_r, b_s, b_r, x_s, x_r, r_s, r_r,
):
    ng = n_mem // nc
    rows, cols = u_ref.shape
    ml = noise_ref.shape[0]
    cc = cols // nc
    ob = noise_ref.shape[1]
    members = n_mem * ml
    me = lax.axis_index("mem")
    sl = lax.axis_index("slab")
    my_g = me // nc
    my_c = me % nc
    up = lax.rem(sl + 1, n_slab)
    down = lax.rem(sl + n_slab - 1, n_slab)

    barrier = pltpu.get_barrier_semaphore()
    for k in range(1, n_mem):
        pl.semaphore_signal(barrier, inc=1, device_id=(lax.rem(me + k, n_mem), sl), device_id_type=MESH)
    for k in range(1, n_slab):
        pl.semaphore_signal(barrier, inc=1, device_id=(me, lax.rem(sl + k, n_slab)), device_id_type=MESH)

    tr = 8

    def load_rows(i, carry):
        r = pl.multiple_of(i * tr, tr)
        t_buf[pl.ds(r + 2, tr)] = jnp.swapaxes(x_ref[:, pl.ds(r, tr), :], 0, 1)
        return carry

    lax.fori_loop(0, rows // tr, load_rows, 0)
    for r in range(2):
        up_buf[r] = t_buf[2 + r]
        dn_buf[r] = t_buf[rows + r]
    up_buf[2] = jnp.broadcast_to(v_ref[pl.ds(0, 1), :], (ml, cols))
    v_buf[0:rows, :] = v_ref[...]

    pl.semaphore_wait(barrier, n_mem - 1 + n_slab - 1)

    def halo_copy(i, src, dst, target):
        return pltpu.make_async_remote_copy(
            src_ref=src, dst_ref=dst, send_sem=halo_s.at[i], recv_sem=halo_r.at[i],
            device_id=(me, target), device_id_type=MESH)

    to_down = halo_copy(0, up_buf, hi_rx, down)
    to_up = halo_copy(1, dn_buf, lo_rx, up)
    to_down.start()
    to_up.start()

    lane = lax.broadcasted_iota(jnp.int32, (ml, cols), 1)
    first_lane = lane == 0
    last_lane = lane == cols - 1

    def from_left(a):
        return jnp.where(first_lane, 0.0, pltpu.roll(a, 1, 1))

    def from_right(a):
        return jnp.where(last_lane, 0.0, pltpu.roll(a, cols - 1, 1))

    def compute(g):
        r0 = g * rc
        hm2, hm1, h0, h1 = (t_buf[r0 + i] for i in range(4))
        s_low = minmod(hm1 - hm2, h0 - hm1)
        s = minmod(h0 - hm1, h1 - h0)
        w = v_buf[pl.ds(r0, 1), :]
        flux = jnp.maximum(w, 0.0) * (hm1 + 0.5 * s_low) + jnp.minimum(w, 0.0) * (h0 - 0.5 * s)
        for r in range(rc):
            h2 = t_buf[r0 + r + 4]
            s1 = minmod(h1 - h0, h2 - h1)
            w = v_buf[pl.ds(r0 + r + 1, 1), :]
            flux1 = jnp.maximum(w, 0.0) * (h0 + 0.5 * s) + jnp.minimum(w, 0.0) * (h1 - 0.5 * s1)
            u = u_ref[pl.ds(r0 + r, 1), :]
            d = h0 - from_left(h0)
            d1 = from_right(h0) - h0
            sc = 0.5 * minmod(d, d1)
            fc = jnp.maximum(u, 0.0) * from_left(h0 + sc) + jnp.minimum(u, 0.0) * (h0 - sc)
            f = h0 - (from_right(fc) - fc) - (flux1 - flux)
            for ci in range(nc):
                fblk[g, ci, r] = f[:, ci * cc:(ci + 1) * cc]
            h0, h1, s, flux = h1, h2, s1, flux1

    def fwd_copy(g, ci, t, slot):
        return pltpu.make_async_remote_copy(
            src_ref=fblk.at[g, ci], dst_ref=gath.at[slot], send_sem=f_s.at[t], recv_sem=f_r.at[slot],
            device_id=(t, sl), device_id_type=MESH)

    def send_group(g):
        for ci in range(nc):
            t = g * nc + ci

            @pl.when(t != me)
            def _():
                fwd_copy(g, ci, t, me).start()

    def inner(k, carry):
        g = lax.rem(my_g + k, ng)

        @pl.when(jnp.logical_and(g >= 1, g <= ng - 2))
        def _():
            compute(g)
            send_group(g)

        return carry

    lax.fori_loop(1, ng + 1, inner, 0)

    base = (sl * (rows * cols)).astype(F32)
    local_cells = cells_ref[...].astype(F32) - base
    cell_row = jnp.floor((local_cells + 0.5) * (1.0 / cols))
    cell_col = local_cells - cell_row * cols
    weights = wts_ref[...].astype(F32)
    w_sum = jnp.sum(weights, axis=0, keepdims=True)
    col_min = jnp.min(cell_col, axis=0, keepdims=True)
    col_iota = lax.broadcasted_iota(jnp.int32, (cols, ob), 0).astype(F32)
    row_iota = lax.broadcasted_iota(jnp.int32, (rows, ob), 0).astype(F32)
    onehot = []
    for b in range(2):
        onehot.append((col_iota == col_min + float(b)).astype(F32))
        total = jnp.zeros((rows, ob), F32)
        for k in range(cells_ref.shape[0]):
            wk = jnp.where(cell_col[k:k + 1] == col_min + float(b), weights[k:k + 1], 0.0)
            total += jnp.where(row_iota == cell_row[k:k + 1], wk, 0.0)
        rw_buf[:, b * ob:(b + 1) * ob] = total
    onehot = jnp.concatenate(onehot, axis=1).astype(BF16)

    to_down.wait_recv()
    to_up.wait_recv()
    low_edge = sl == 0
    high_edge = sl == n_slab - 1
    for r in range(2):
        t_buf[r] = jnp.where(low_edge, 0.0, lo_rx[r])
        t_buf[rows + 2 + r] = jnp.where(high_edge, 0.0, hi_rx[r])
    v_buf[rows:rows + 8, :] = jnp.broadcast_to(jnp.where(high_edge, 0.0, hi_rx[2])[0:1], (8, cols))
    compute(0)
    compute(ng - 1)

    s_total = None
    for ci in range(nc):
        f = fblk[:, ci].reshape(rows * ml, cc)
        f_hi = f.astype(BF16)
        f_lo = (f - f_hi.astype(F32)).astype(BF16)
        q = onehot[ci * cc:(ci + 1) * cc]
        part = jnp.dot(f_hi, q, preferred_element_type=F32) + jnp.dot(f_lo, q, preferred_element_type=F32)
        s_total = part if s_total is None else s_total + part
    s_buf[...] = s_total

    acc = jnp.zeros((ml, 2 * ob), F32)
    for r in range(rows):
        acc += s_buf[r * ml:(r + 1) * ml, :] * rw_buf[r:r + 1, :]
    obs_model = (acc[:, :ob] + acc[:, ob:]) / w_sum
    om_all[me] = obs_model

    def bcast(buf, slot, i, t_mem, t_slab, ss, rs):
        return pltpu.make_async_remote_copy(
            src_ref=buf.at[slot], dst_ref=buf.at[slot], send_sem=ss.at[i], recv_sem=rs.at[slot],
            device_id=(t_mem, t_slab), device_id_type=MESH)

    mem_mates = [lax.rem(me + k, n_mem) for k in range(1, n_mem)]
    slab_mates = [lax.rem(sl + k, n_slab) for k in range(1, n_slab)]

    for t in mem_mates:
        bcast(om_all, me, t, t, sl, o_s, o_r).start()

    innovation = vals_ref[...] + noise_ref[...] - obs_model
    white_terms = jnp.dot(innovation, cinv_ref[...], preferred_element_type=F32, precision=lax.Precision.HIGHEST)
    for b in range(n_slab):
        p_buf[b] = white_terms[:, b * ob:(b + 1) * ob]
    p_rx[sl] = p_buf[sl]

    def p_copy(b, slot):
        return pltpu.make_async_remote_copy(
            src_ref=p_buf.at[b], dst_ref=p_rx.at[slot], send_sem=p_s.at[b], recv_sem=p_r.at[slot],
            device_id=(me, b), device_id_type=MESH)

    for b in slab_mates:
        p_copy(b, sl).start()

    send_group(0)
    send_group(ng - 1)
    gath[me] = fblk[my_g, my_c]

    for b in slab_mates:
        p_copy(b, b).wait_recv()
    whitened = p_rx[0]
    for b in range(1, n_slab):
        whitened += p_rx[b]
    for t in mem_mates:
        bcast(om_all, t, t, t, sl, o_s, o_r).wait_recv()
    om = om_all[...].reshape(members, ob)
    obs_anomaly = om - jnp.sum(om, axis=0, keepdims=True) * (1.0 / members)
    b_buf[sl] = lax.dot_general(
        whitened, obs_anomaly, (((1,), (1,)), ((), ())),
        preferred_element_type=F32, precision=lax.Precision.HIGHEST)
    for b in slab_mates:
        bcast(b_buf, sl, b, me, b, b_s, b_r).start()
    for b in slab_mates:
        bcast(b_buf, b, b, me, b, b_s, b_r).wait_recv()
    ens = jnp.zeros((ml, members), F32)
    for b in range(n_slab):
        ens += taper_ref[sl, b].astype(F32) * b_buf[b]
    ens = ens - jnp.sum(ens, axis=1, keepdims=True) * (1.0 / members)
    x_all[me] = ens * (1.0 / (members - 1))
    for t in mem_mates:
        bcast(x_all, me, t, t, sl, x_s, x_r).start()

    for t in mem_mates:
        fwd_copy(my_g, my_c, t, t).wait_recv()
    for t in mem_mates:
        bcast(x_all, t, t, t, sl, x_s, x_r).wait_recv()

    xm = x_all[...].reshape(members, members)
    x_hi = xm.astype(BF16).astype(F32)
    lhs = jnp.concatenate([x_hi, x_hi, xm - x_hi], axis=1).astype(BF16)
    for r in range(rc):
        g = gath[:, r].reshape(members, cc)
        g_hi = g.astype(BF16)
        g_lo = (g - g_hi.astype(F32)).astype(BF16)
        rhs = jnp.concatenate([g_hi, g_lo, g_hi], axis=0)
        out = g + jnp.dot(lhs, rhs, preferred_element_type=F32)
        outb[:, r] = out.reshape(n_mem, ml, cc)

    def rev_copy(t, g, ci, slot):
        return pltpu.make_async_remote_copy(
            src_ref=outb.at[t], dst_ref=res_ref.at[g, ci], send_sem=r_s.at[t], recv_sem=r_r.at[slot],
            device_id=(t, sl), device_id_type=MESH)

    for t in mem_mates:
        rev_copy(t, my_g, my_c, me).start()
    res_ref[my_g, my_c] = outb[me]

    to_down.wait_send()
    to_up.wait_send()
    for b in slab_mates:
        p_copy(b, sl).wait_send()
        bcast(b_buf, sl, b, me, b, b_s, b_r).wait_send()
    for t in mem_mates:
        bcast(om_all, me, t, t, sl, o_s, o_r).wait_send()
        bcast(x_all, me, t, t, sl, x_s, x_r).wait_send()
        fwd_copy(t // nc, t % nc, t, me).wait_send()
    for t in mem_mates:
        rev_copy(t, my_g, my_c, me).wait_send()
    for t in mem_mates:
        rev_copy(t, t // nc, t % nc, t).wait_recv()


def local(n_mem, n_slab, thickness, face_u, face_v, obs_cells, obs_weights, obs_values, obs_noise, cov_inverse,
          taper_mask):
    ml, rows, cols = thickness.shape
    ob = obs_values.shape[0]
    members = ml * n_mem
    nc, rc = split_blocks(rows, cols, n_mem)
    ng, cc = n_mem // nc, cols // nc
    vmem = pl.BlockSpec(memory_space=pltpu.VMEM)
    dma = pltpu.SemaphoreType.DMA
    out = pl.pallas_call(
        functools.partial(kernel, n_mem, n_slab, nc, rc),
        out_shape=jax.ShapeDtypeStruct((ng, nc, rc, ml, cc), F32),
        in_specs=[vmem] * 8 + [pl.BlockSpec(memory_space=pltpu.SMEM)],
        out_specs=vmem,
        scratch_shapes=[
            pltpu.VMEM((rows + 4, ml, cols), F32),
            pltpu.VMEM((rows + 8, cols), F32),
            pltpu.VMEM((3, ml, cols), F32),
            pltpu.VMEM((2, ml, cols), F32),
            pltpu.VMEM((3, ml, cols), F32),
            pltpu.VMEM((2, ml, cols), F32),
            pltpu.VMEM((ng, nc, rc, ml, cc), F32),
            pltpu.VMEM((n_mem, rc, ml, cc), F32),
            pltpu.VMEM((n_mem, rc, ml, cc), F32),
            pltpu.VMEM((rows * ml, 2 * ob), F32),
            pltpu.VMEM((rows, 2 * ob), F32),
            pltpu.VMEM((n_mem, ml, ob), F32),
            pltpu.VMEM((n_slab, ml, ob), F32),
            pltpu.VMEM((n_slab, ml, ob), F32),
            pltpu.VMEM((n_slab, ml, members), F32),
            pltpu.VMEM((n_mem, ml, members), F32),
            dma((2,)), dma((2,)),
            dma((n_mem,)), dma((n_mem,)),
            dma((n_mem,)), dma((n_mem,)),
            dma((n_slab,)), dma((n_slab,)),
            dma((n_slab,)), dma((n_slab,)),
            dma((n_mem,)), dma((n_mem,)),
            dma((n_mem,)), dma((n_mem,)),
        ],
        compiler_params=pltpu.CompilerParams(collective_id=0, has_side_effects=True),
    )(
        thickness, face_u, face_v, obs_cells.T, obs_weights.T,
        obs_values.reshape(1, ob), obs_noise, cov_inverse, taper_mask,
    )
    return out.transpose(3, 0, 2, 1, 4).reshape(ml, rows, cols)


def solution(mesh):
    return jax.shard_map(
        functools.partial(local, mesh.shape["mem"], mesh.shape["slab"]),
        mesh=mesh,
        in_specs=(
            P("mem", "slab", None),
            P("slab", None),
            P("slab", None),
            P("slab", None),
            P("slab", None),
            P("slab"),
            P("mem", "slab"),
            P("slab", None),
            P(),
        ),
        out_specs=P("mem", "slab", None),
        check_vma=False,
    )
```

```python
import functools

import jax
import jax.numpy as jnp
from jax import lax
from jax.experimental import pallas as pl
from jax.experimental.pallas import tpu as pltpu
from jax.sharding import PartitionSpec as P

MESH = pl.DeviceIdType.MESH
F32 = jnp.float32
BF16 = jnp.bfloat16


def minmod(a, b):
    return jnp.maximum(jnp.minimum(a, b), 0.0) + jnp.minimum(jnp.maximum(a, b), 0.0)


def split_blocks(rows, cols, n_mem):
    for nc in range(1, n_mem + 1):
        if n_mem % nc == 0 and cols % (128 * nc) == 0 and rows % (n_mem // nc) == 0:
            return nc, rows // (n_mem // nc)
    raise ValueError("no split")


def kernel(
    n_mem, n_slab, nc, rc, ck,
    x_hbm, u_ref, v_ref, cells_ref, wts_ref, vals_ref, noise_ref, cinv_hbm, taper_ref,
    res_ref,
    t_buf, v_buf, up_buf, dn_buf, hi_rx, lo_rx, fblk, gath, outb, s_buf, rw_buf,
    om_all, p_buf, p_rx, b_buf, x_all, x_ref, cinv_ref, in_s,
    halo_s, halo_r, f_s, f_r, o_s, o_r, p_s, p_r, b_s, b_r, x_s, x_r, r_s, r_r,
):
    ng = n_mem // nc
    rows, cols = u_ref.shape
    ml = noise_ref.shape[0]
    cc = cols // nc
    ob = noise_ref.shape[1]
    members = n_mem * ml
    me = lax.axis_index("mem")
    sl = lax.axis_index("slab")
    my_g = me // nc
    my_c = me % nc
    up = lax.rem(sl + 1, n_slab)
    down = lax.rem(sl + n_slab - 1, n_slab)

    nch = rc // ck

    x_in = pltpu.make_async_copy(x_hbm, x_ref, in_s.at[0])
    cinv_in = pltpu.make_async_copy(cinv_hbm, cinv_ref, in_s.at[1])
    x_in.start()
    cinv_in.start()

    barrier = pltpu.get_barrier_semaphore()
    for k in range(1, n_mem):
        pl.semaphore_signal(barrier, inc=1, device_id=(lax.rem(me + k, n_mem), sl), device_id_type=MESH)
    for k in range(1, n_slab):
        pl.semaphore_signal(barrier, inc=1, device_id=(me, lax.rem(sl + k, n_slab)), device_id_type=MESH)

    x_in.wait()
    tr = 8

    def load_rows(i, carry):
        r = pl.multiple_of(i * tr, tr)
        t_buf[pl.ds(r + 2, tr)] = jnp.swapaxes(x_ref[:, pl.ds(r, tr), :], 0, 1)
        return carry

    lax.fori_loop(0, rows // tr, load_rows, 0)
    for r in range(2):
        up_buf[r] = t_buf[2 + r]
        dn_buf[r] = t_buf[rows + r]
    up_buf[2] = jnp.broadcast_to(v_ref[pl.ds(0, 1), :], (ml, cols))
    v_buf[0:rows, :] = v_ref[...]

    pl.semaphore_wait(barrier, n_mem - 1 + n_slab - 1)

    def halo_copy(i, src, dst, target):
        return pltpu.make_async_remote_copy(
            src_ref=src, dst_ref=dst, send_sem=halo_s.at[i], recv_sem=halo_r.at[i],
            device_id=(me, target), device_id_type=MESH)

    to_down = halo_copy(0, up_buf, hi_rx, down)
    to_up = halo_copy(1, dn_buf, lo_rx, up)
    to_down.start()
    to_up.start()

    lane = lax.broadcasted_iota(jnp.int32, (ml, cols), 1)
    first_lane = lane == 0
    last_lane = lane == cols - 1

    def from_left(a):
        return jnp.where(first_lane, 0.0, pltpu.roll(a, 1, 1))

    def from_right(a):
        return jnp.where(last_lane, 0.0, pltpu.roll(a, cols - 1, 1))

    def compute(g):
        r0 = g * rc
        hm2, hm1, h0, h1 = (t_buf[r0 + i] for i in range(4))
        s_low = minmod(hm1 - hm2, h0 - hm1)
        s = minmod(h0 - hm1, h1 - h0)
        w = v_buf[pl.ds(r0, 1), :]
        flux = jnp.maximum(w, 0.0) * (hm1 + 0.5 * s_low) + jnp.minimum(w, 0.0) * (h0 - 0.5 * s)
        for r in range(rc):
            h2 = t_buf[r0 + r + 4]
            s1 = minmod(h1 - h0, h2 - h1)
            w = v_buf[pl.ds(r0 + r + 1, 1), :]
            flux1 = jnp.maximum(w, 0.0) * (h0 + 0.5 * s) + jnp.minimum(w, 0.0) * (h1 - 0.5 * s1)
            u = u_ref[pl.ds(r0 + r, 1), :]
            d = h0 - from_left(h0)
            d1 = from_right(h0) - h0
            sc = 0.5 * minmod(d, d1)
            fc = jnp.maximum(u, 0.0) * from_left(h0 + sc) + jnp.minimum(u, 0.0) * (h0 - sc)
            f = h0 - (from_right(fc) - fc) - (flux1 - flux)
            for ci in range(nc):
                fblk[g, ci, r] = f[:, ci * cc:(ci + 1) * cc]
            h0, h1, s, flux = h1, h2, s1, flux1

    def chunk(k):
        return pl.ds(k * ck, ck)

    def fwd_copy(k, g, ci, t, slot):
        return pltpu.make_async_remote_copy(
            src_ref=fblk.at[g, ci, chunk(k)], dst_ref=gath.at[slot, chunk(k)],
            send_sem=f_s.at[k, t], recv_sem=f_r.at[k, slot], device_id=(t, sl), device_id_type=MESH)

    def send_group(g, k):
        for ci in range(nc):
            t = g * nc + ci

            @pl.when(t != me)
            def _():
                fwd_copy(k, g, ci, t, me).start()

    def inner(k, carry):
        g = lax.rem(my_g + k, ng)

        @pl.when(jnp.logical_and(g >= 1, g <= ng - 2))
        def _():
            compute(g)
            send_group(g, 0)

        return carry

    lax.fori_loop(1, ng + 1, inner, 0)

    base = (sl * (rows * cols)).astype(F32)
    local_cells = cells_ref[...].astype(F32) - base
    cell_row = jnp.floor((local_cells + 0.5) * (1.0 / cols))
    cell_col = local_cells - cell_row * cols
    weights = wts_ref[...].astype(F32)
    w_sum = jnp.sum(weights, axis=0, keepdims=True)
    col_min = jnp.min(cell_col, axis=0, keepdims=True)
    col_iota = lax.broadcasted_iota(jnp.int32, (cols, ob), 0).astype(F32)
    row_iota = lax.broadcasted_iota(jnp.int32, (rows, ob), 0).astype(F32)
    onehot = []
    for b in range(2):
        onehot.append((col_iota == col_min + float(b)).astype(F32))
        total = jnp.zeros((rows, ob), F32)
        for k in range(cells_ref.shape[0]):
            wk = jnp.where(cell_col[k:k + 1] == col_min + float(b), weights[k:k + 1], 0.0)
            total += jnp.where(row_iota == cell_row[k:k + 1], wk, 0.0)
        rw_buf[:, b * ob:(b + 1) * ob] = total
    onehot = jnp.concatenate(onehot, axis=1).astype(BF16)

    to_down.wait_recv()
    to_up.wait_recv()
    low_edge = sl == 0
    high_edge = sl == n_slab - 1
    for r in range(2):
        t_buf[r] = jnp.where(low_edge, 0.0, lo_rx[r])
        t_buf[rows + 2 + r] = jnp.where(high_edge, 0.0, hi_rx[r])
    v_buf[rows:rows + 8, :] = jnp.broadcast_to(jnp.where(high_edge, 0.0, hi_rx[2])[0:1], (8, cols))
    compute(0)
    compute(ng - 1)

    s_total = None
    for ci in range(nc):
        f = fblk[:, ci].reshape(rows * ml, cc)
        f_hi = f.astype(BF16)
        f_lo = (f - f_hi.astype(F32)).astype(BF16)
        q = onehot[ci * cc:(ci + 1) * cc]
        part = jnp.dot(f_hi, q, preferred_element_type=F32) + jnp.dot(f_lo, q, preferred_element_type=F32)
        s_total = part if s_total is None else s_total + part
    s_buf[...] = s_total

    acc = jnp.zeros((ml, 2 * ob), F32)
    for r in range(rows):
        acc += s_buf[r * ml:(r + 1) * ml, :] * rw_buf[r:r + 1, :]
    obs_model = (acc[:, :ob] + acc[:, ob:]) / w_sum
    om_all[me] = obs_model

    def bcast(buf, slot, i, t_mem, t_slab, ss, rs):
        return pltpu.make_async_remote_copy(
            src_ref=buf.at[slot], dst_ref=buf.at[slot], send_sem=ss.at[i], recv_sem=rs.at[slot],
            device_id=(t_mem, t_slab), device_id_type=MESH)

    mem_mates = [lax.rem(me + k, n_mem) for k in range(1, n_mem)]
    slab_mates = [lax.rem(sl + k, n_slab) for k in range(1, n_slab)]

    for t in mem_mates:
        bcast(om_all, me, t, t, sl, o_s, o_r).start()

    innovation = vals_ref[...] + noise_ref[...] - obs_model
    cinv_in.wait()
    white_terms = jnp.dot(innovation, cinv_ref[...], preferred_element_type=F32, precision=lax.Precision.HIGHEST)
    for b in range(n_slab):
        p_buf[b] = white_terms[:, b * ob:(b + 1) * ob]
    p_rx[sl] = p_buf[sl]

    def p_copy(b, slot):
        return pltpu.make_async_remote_copy(
            src_ref=p_buf.at[b], dst_ref=p_rx.at[slot], send_sem=p_s.at[b], recv_sem=p_r.at[slot],
            device_id=(me, b), device_id_type=MESH)

    for b in slab_mates:
        p_copy(b, sl).start()

    send_group(0, 0)
    send_group(ng - 1, 0)

    def send_chunk(k):
        for t in mem_mates:
            fwd_copy(k, t // nc, t % nc, t, me).start()

    if nch > 1:
        send_chunk(1)
    gath[me] = fblk[my_g, my_c]

    for b in slab_mates:
        p_copy(b, b).wait_recv()
    whitened = p_rx[0]
    for b in range(1, n_slab):
        whitened += p_rx[b]
    for t in mem_mates:
        bcast(om_all, t, t, t, sl, o_s, o_r).wait_recv()
    om = om_all[...].reshape(members, ob)
    obs_anomaly = om - jnp.sum(om, axis=0, keepdims=True) * (1.0 / members)
    b_buf[sl] = lax.dot_general(
        whitened, obs_anomaly, (((1,), (1,)), ((), ())),
        preferred_element_type=F32, precision=lax.Precision.HIGHEST)
    for b in slab_mates:
        bcast(b_buf, sl, b, me, b, b_s, b_r).start()
    for b in slab_mates:
        bcast(b_buf, b, b, me, b, b_s, b_r).wait_recv()
    ens = jnp.zeros((ml, members), F32)
    for b in range(n_slab):
        ens += taper_ref[sl, b].astype(F32) * b_buf[b]
    ens = ens - jnp.sum(ens, axis=1, keepdims=True) * (1.0 / members)
    x_all[me] = ens * (1.0 / (members - 1))
    for t in mem_mates:
        bcast(x_all, me, t, t, sl, x_s, x_r).start()

    for k in range(2, nch):
        send_chunk(k)

    for t in mem_mates:
        bcast(x_all, t, t, t, sl, x_s, x_r).wait_recv()
    xm = x_all[...].reshape(members, members)
    x_hi = xm.astype(BF16).astype(F32)
    lhs = jnp.concatenate([x_hi, x_hi, xm - x_hi], axis=1).astype(BF16)

    def rev_copy(k, t, g, ci, slot):
        return pltpu.make_async_remote_copy(
            src_ref=outb.at[t, chunk(k)], dst_ref=res_ref.at[g, ci, chunk(k)],
            send_sem=r_s.at[k, t], recv_sem=r_r.at[k, slot], device_id=(t, sl), device_id_type=MESH)

    for k in range(nch):
        for t in mem_mates:
            fwd_copy(k, my_g, my_c, t, t).wait_recv()
        for r in range(k * ck, (k + 1) * ck):
            g = gath[:, r].reshape(members, cc)
            g_hi = g.astype(BF16)
            g_lo = (g - g_hi.astype(F32)).astype(BF16)
            rhs = jnp.concatenate([g_hi, g_lo, g_hi], axis=0)
            out = g + jnp.dot(lhs, rhs, preferred_element_type=F32)
            outb[:, r] = out.reshape(n_mem, ml, cc)
        for t in mem_mates:
            rev_copy(k, t, my_g, my_c, me).start()
    res_ref[my_g, my_c] = outb[me]

    to_down.wait_send()
    to_up.wait_send()
    for b in slab_mates:
        p_copy(b, sl).wait_send()
        bcast(b_buf, sl, b, me, b, b_s, b_r).wait_send()
    for t in mem_mates:
        bcast(om_all, me, t, t, sl, o_s, o_r).wait_send()
        bcast(x_all, me, t, t, sl, x_s, x_r).wait_send()
        for k in range(nch):
            fwd_copy(k, t // nc, t % nc, t, me).wait_send()
    for k in range(nch):
        for t in mem_mates:
            rev_copy(k, t, my_g, my_c, me).wait_send()
        for t in mem_mates:
            rev_copy(k, t, t // nc, t % nc, t).wait_recv()


def local(n_mem, n_slab, thickness, face_u, face_v, obs_cells, obs_weights, obs_values, obs_noise, cov_inverse,
          taper_mask):
    ml, rows, cols = thickness.shape
    ob = obs_values.shape[0]
    members = ml * n_mem
    nc, rc = split_blocks(rows, cols, n_mem)
    ng, cc = n_mem // nc, cols // nc
    ck = rc // 4 if rc % 4 == 0 else rc
    nch = rc // ck
    vmem = pl.BlockSpec(memory_space=pltpu.VMEM)
    hbm = pl.BlockSpec(memory_space=pl.ANY)
    dma = pltpu.SemaphoreType.DMA
    out = pl.pallas_call(
        functools.partial(kernel, n_mem, n_slab, nc, rc, ck),
        out_shape=jax.ShapeDtypeStruct((ng, nc, rc, ml, cc), F32),
        in_specs=[hbm] + [vmem] * 6 + [hbm, pl.BlockSpec(memory_space=pltpu.SMEM)],
        out_specs=vmem,
        scratch_shapes=[
            pltpu.VMEM((rows + 4, ml, cols), F32),
            pltpu.VMEM((rows + 8, cols), F32),
            pltpu.VMEM((3, ml, cols), F32),
            pltpu.VMEM((2, ml, cols), F32),
            pltpu.VMEM((3, ml, cols), F32),
            pltpu.VMEM((2, ml, cols), F32),
            pltpu.VMEM((ng, nc, rc, ml, cc), F32),
            pltpu.VMEM((n_mem, rc, ml, cc), F32),
            pltpu.VMEM((n_mem, rc, ml, cc), F32),
            pltpu.VMEM((rows * ml, 2 * ob), F32),
            pltpu.VMEM((rows, 2 * ob), F32),
            pltpu.VMEM((n_mem, ml, ob), F32),
            pltpu.VMEM((n_slab, ml, ob), F32),
            pltpu.VMEM((n_slab, ml, ob), F32),
            pltpu.VMEM((n_slab, ml, members), F32),
            pltpu.VMEM((n_mem, ml, members), F32),
            pltpu.VMEM((ml, rows, cols), F32),
            pltpu.VMEM((ob, n_slab * ob), F32),
            dma((2,)),
            dma((2,)), dma((2,)),
            dma((nch, n_mem)), dma((nch, n_mem)),
            dma((n_mem,)), dma((n_mem,)),
            dma((n_slab,)), dma((n_slab,)),
            dma((n_slab,)), dma((n_slab,)),
            dma((n_mem,)), dma((n_mem,)),
            dma((nch, n_mem)), dma((nch, n_mem)),
        ],
        compiler_params=pltpu.CompilerParams(collective_id=0, has_side_effects=True),
    )(
        thickness, face_u, face_v, obs_cells.T, obs_weights.T,
        obs_values.reshape(1, ob), obs_noise, cov_inverse, taper_mask,
    )
    return out.transpose(3, 0, 2, 1, 4).reshape(ml, rows, cols)


def solution(mesh):
    return jax.shard_map(
        functools.partial(local, mesh.shape["mem"], mesh.shape["slab"]),
        mesh=mesh,
        in_specs=(
            P("mem", "slab", None),
            P("slab", None),
            P("slab", None),
            P("slab", None),
            P("slab", None),
            P("slab"),
            P("mem", "slab"),
            P("slab", None),
            P(),
        ),
        out_specs=P("mem", "slab", None),
        check_vma=False,
    )
```

```python
import functools

import jax
import jax.numpy as jnp
from jax import lax
from jax.experimental import pallas as pl
from jax.experimental.pallas import tpu as pltpu
from jax.sharding import PartitionSpec as P

MESH = pl.DeviceIdType.MESH
F32 = jnp.float32
BF16 = jnp.bfloat16


def minmod(a, b):
    return jnp.maximum(jnp.minimum(a, b), 0.0) + jnp.minimum(jnp.maximum(a, b), 0.0)


def split_blocks(rows, cols, n_mem):
    for nc in range(1, n_mem + 1):
        if n_mem % nc == 0 and cols % (128 * nc) == 0 and rows % (n_mem // nc) == 0:
            return nc, rows // (n_mem // nc)
    raise ValueError("no split")


def kernel(
    n_mem, n_slab, nc, rc, ck,
    x_hbm, u_ref, v_ref, cells_ref, wts_ref, vals_ref, noise_ref, cinv_hbm, taper_ref,
    res_ref,
    t_buf, v_buf, up_buf, dn_buf, hi_rx, lo_rx, fblk, gath, outb, s_buf, rw_buf,
    om_all, p_buf, p_rx, b_buf, x_all, x_ref, cinv_ref, in_s,
    halo_s, halo_r, f_s, f_r, o_s, o_r, p_s, p_r, b_s, b_r, x_s, x_r, r_s, r_r,
):
    ng = n_mem // nc
    rows, cols = u_ref.shape
    ml = noise_ref.shape[0]
    cc = cols // nc
    ob = noise_ref.shape[1]
    members = n_mem * ml
    me = lax.axis_index("mem")
    sl = lax.axis_index("slab")
    my_g = me // nc
    my_c = me % nc
    up = lax.rem(sl + 1, n_slab)
    down = lax.rem(sl + n_slab - 1, n_slab)

    nch = rc // ck

    x_in = pltpu.make_async_copy(x_hbm, x_ref, in_s.at[0])
    cinv_in = pltpu.make_async_copy(cinv_hbm, cinv_ref, in_s.at[1])
    x_in.start()
    cinv_in.start()

    barrier = pltpu.get_barrier_semaphore()
    for k in range(1, n_mem):
        pl.semaphore_signal(barrier, inc=1, device_id=(lax.rem(me + k, n_mem), sl), device_id_type=MESH)
    for k in range(1, n_slab):
        pl.semaphore_signal(barrier, inc=1, device_id=(me, lax.rem(sl + k, n_slab)), device_id_type=MESH)

    x_in.wait()
    tr = 8

    def load_rows(i, carry):
        r = pl.multiple_of(i * tr, tr)
        t_buf[pl.ds(r + 2, tr)] = jnp.swapaxes(x_ref[:, pl.ds(r, tr), :], 0, 1)
        return carry

    lax.fori_loop(0, rows // tr, load_rows, 0)
    for r in range(2):
        up_buf[r] = t_buf[2 + r]
        dn_buf[r] = t_buf[rows + r]
    up_buf[2] = jnp.broadcast_to(v_ref[pl.ds(0, 1), :], (ml, cols))
    v_buf[0:rows, :] = v_ref[...]

    pl.semaphore_wait(barrier, n_mem - 1 + n_slab - 1)

    def halo_copy(i, src, dst, target):
        return pltpu.make_async_remote_copy(
            src_ref=src, dst_ref=dst, send_sem=halo_s.at[i], recv_sem=halo_r.at[i],
            device_id=(me, target), device_id_type=MESH)

    to_down = halo_copy(0, up_buf, hi_rx, down)
    to_up = halo_copy(1, dn_buf, lo_rx, up)
    to_down.start()
    to_up.start()

    lane = lax.broadcasted_iota(jnp.int32, (ml, cols), 1)
    first_lane = lane == 0
    last_lane = lane == cols - 1

    def from_left(a):
        return jnp.where(first_lane, 0.0, pltpu.roll(a, 1, 1))

    def from_right(a):
        return jnp.where(last_lane, 0.0, pltpu.roll(a, cols - 1, 1))

    def compute(g):
        r0 = g * rc
        hm2, hm1, h0, h1 = (t_buf[r0 + i] for i in range(4))
        s_low = minmod(hm1 - hm2, h0 - hm1)
        s = minmod(h0 - hm1, h1 - h0)
        w = v_buf[pl.ds(r0, 1), :]
        flux = jnp.maximum(w, 0.0) * (hm1 + 0.5 * s_low) + jnp.minimum(w, 0.0) * (h0 - 0.5 * s)
        for r in range(rc):
            h2 = t_buf[r0 + r + 4]
            s1 = minmod(h1 - h0, h2 - h1)
            w = v_buf[pl.ds(r0 + r + 1, 1), :]
            flux1 = jnp.maximum(w, 0.0) * (h0 + 0.5 * s) + jnp.minimum(w, 0.0) * (h1 - 0.5 * s1)
            u = u_ref[pl.ds(r0 + r, 1), :]
            d = h0 - from_left(h0)
            d1 = from_right(h0) - h0
            sc = 0.5 * minmod(d, d1)
            fc = jnp.maximum(u, 0.0) * from_left(h0 + sc) + jnp.minimum(u, 0.0) * (h0 - sc)
            f = h0 - (from_right(fc) - fc) - (flux1 - flux)
            for ci in range(nc):
                fblk[g, ci, r] = f[:, ci * cc:(ci + 1) * cc]
            h0, h1, s, flux = h1, h2, s1, flux1

    def chunk(k):
        return pl.ds(k * ck, ck)

    def fwd_copy(k, g, ci, t, slot):
        return pltpu.make_async_remote_copy(
            src_ref=fblk.at[g, ci, chunk(k)], dst_ref=gath.at[slot, chunk(k)],
            send_sem=f_s.at[k, t], recv_sem=f_r.at[k, slot], device_id=(t, sl), device_id_type=MESH)

    def send_group(g, k):
        for ci in range(nc):
            t = g * nc + ci

            @pl.when(t != me)
            def _():
                fwd_copy(k, g, ci, t, me).start()

    def inner(k, carry):
        g = lax.rem(my_g + k, ng)

        @pl.when(jnp.logical_and(g >= 1, g <= ng - 2))
        def _():
            compute(g)
            send_group(g, 0)

        return carry

    lax.fori_loop(1, ng + 1, inner, 0)

    base = (sl * (rows * cols)).astype(F32)
    local_cells = cells_ref[...].astype(F32) - base
    cell_row = jnp.floor((local_cells + 0.5) * (1.0 / cols))
    cell_col = local_cells - cell_row * cols
    weights = wts_ref[...].astype(F32)
    w_sum = jnp.sum(weights, axis=0, keepdims=True)
    col_min = jnp.min(cell_col, axis=0, keepdims=True)
    col_iota = lax.broadcasted_iota(jnp.int32, (cols, ob), 0).astype(F32)
    row_iota = lax.broadcasted_iota(jnp.int32, (rows, ob), 0).astype(F32)
    onehot = []
    for b in range(2):
        onehot.append((col_iota == col_min + float(b)).astype(F32))
        total = jnp.zeros((rows, ob), F32)
        for k in range(cells_ref.shape[0]):
            wk = jnp.where(cell_col[k:k + 1] == col_min + float(b), weights[k:k + 1], 0.0)
            total += jnp.where(row_iota == cell_row[k:k + 1], wk, 0.0)
        rw_buf[:, b * ob:(b + 1) * ob] = total
    onehot = jnp.concatenate(onehot, axis=1).astype(BF16)

    to_down.wait_recv()
    to_up.wait_recv()
    low_edge = sl == 0
    high_edge = sl == n_slab - 1
    for r in range(2):
        t_buf[r] = jnp.where(low_edge, 0.0, lo_rx[r])
        t_buf[rows + 2 + r] = jnp.where(high_edge, 0.0, hi_rx[r])
    v_buf[rows:rows + 8, :] = jnp.broadcast_to(jnp.where(high_edge, 0.0, hi_rx[2])[0:1], (8, cols))
    compute(0)
    compute(ng - 1)

    s_total = None
    for ci in range(nc):
        f = fblk[:, ci].reshape(rows * ml, cc)
        f_hi = f.astype(BF16)
        f_lo = (f - f_hi.astype(F32)).astype(BF16)
        q = onehot[ci * cc:(ci + 1) * cc]
        part = jnp.dot(f_hi, q, preferred_element_type=F32) + jnp.dot(f_lo, q, preferred_element_type=F32)
        s_total = part if s_total is None else s_total + part
    s_buf[...] = s_total

    acc = jnp.zeros((ml, 2 * ob), F32)
    for r in range(rows):
        acc += s_buf[r * ml:(r + 1) * ml, :] * rw_buf[r:r + 1, :]
    obs_model = (acc[:, :ob] + acc[:, ob:]) / w_sum
    om_all[me] = obs_model

    def bcast(buf, slot, i, t_mem, t_slab, ss, rs):
        return pltpu.make_async_remote_copy(
            src_ref=buf.at[slot], dst_ref=buf.at[slot], send_sem=ss.at[i], recv_sem=rs.at[slot],
            device_id=(t_mem, t_slab), device_id_type=MESH)

    mem_mates = [lax.rem(me + k, n_mem) for k in range(1, n_mem)]
    slab_mates = [lax.rem(sl + k, n_slab) for k in range(1, n_slab)]

    for t in mem_mates:
        bcast(om_all, me, t, t, sl, o_s, o_r).start()

    innovation = vals_ref[...] + noise_ref[...] - obs_model
    cinv_in.wait()
    white_terms = jnp.dot(innovation, cinv_ref[...], preferred_element_type=F32, precision=lax.Precision.HIGHEST)
    for b in range(n_slab):
        p_buf[b] = white_terms[:, b * ob:(b + 1) * ob]
    p_rx[sl] = p_buf[sl]

    def p_copy(b, slot):
        return pltpu.make_async_remote_copy(
            src_ref=p_buf.at[b], dst_ref=p_rx.at[slot], send_sem=p_s.at[b], recv_sem=p_r.at[slot],
            device_id=(me, b), device_id_type=MESH)

    for b in slab_mates:
        p_copy(b, sl).start()

    send_group(0, 0)
    send_group(ng - 1, 0)

    def send_chunk(k):
        for t in mem_mates:
            fwd_copy(k, t // nc, t % nc, t, me).start()

    if nch > 1:
        send_chunk(1)
    gath[me] = fblk[my_g, my_c]

    for b in slab_mates:
        p_copy(b, b).wait_recv()
    whitened = p_rx[0]
    for b in range(1, n_slab):
        whitened += p_rx[b]
    for t in mem_mates:
        bcast(om_all, t, t, t, sl, o_s, o_r).wait_recv()
    om = om_all[...].reshape(members, ob)
    obs_anomaly = om - jnp.sum(om, axis=0, keepdims=True) * (1.0 / members)
    b_buf[sl] = lax.dot_general(
        whitened, obs_anomaly, (((1,), (1,)), ((), ())),
        preferred_element_type=F32, precision=lax.Precision.HIGHEST)
    for b in slab_mates:
        bcast(b_buf, sl, b, me, b, b_s, b_r).start()
    for b in slab_mates:
        bcast(b_buf, b, b, me, b, b_s, b_r).wait_recv()
    ens = jnp.zeros((ml, members), F32)
    for b in range(n_slab):
        ens += taper_ref[sl, b].astype(F32) * b_buf[b]
    ens = ens - jnp.sum(ens, axis=1, keepdims=True) * (1.0 / members)
    x_all[me] = ens * (1.0 / (members - 1))
    for t in mem_mates:
        bcast(x_all, me, t, t, sl, x_s, x_r).start()

    for k in range(2, nch):
        send_chunk(k)

    for t in mem_mates:
        bcast(x_all, t, t, t, sl, x_s, x_r).wait_recv()
    xm = x_all[...].reshape(members, members)
    x_hi = xm.astype(BF16).astype(F32)
    lhs = jnp.concatenate([x_hi, x_hi, xm - x_hi], axis=1).astype(BF16)

    def rev_copy(k, t, g, ci, slot):
        return pltpu.make_async_remote_copy(
            src_ref=outb.at[t, chunk(k)], dst_ref=res_ref.at[g, ci, chunk(k)],
            send_sem=r_s.at[k, t], recv_sem=r_r.at[k, slot], device_id=(t, sl), device_id_type=MESH)

    for k in range(nch):
        for t in mem_mates:
            fwd_copy(k, my_g, my_c, t, t).wait_recv()
        for r in range(k * ck, (k + 1) * ck):
            g = gath[:, r].reshape(members, cc)
            g_hi = g.astype(BF16)
            g_lo = (g - g_hi.astype(F32)).astype(BF16)
            rhs = jnp.concatenate([g_hi, g_lo, g_hi], axis=0)
            out = g + jnp.dot(lhs, rhs, preferred_element_type=F32)
            outb[:, r] = out.reshape(n_mem, ml, cc)
        for t in mem_mates:
            rev_copy(k, t, my_g, my_c, me).start()
    own = pltpu.make_async_copy(outb.at[me], res_ref.at[my_g, my_c], in_s.at[0])
    own.start()
    own.wait()

    to_down.wait_send()
    to_up.wait_send()
    for b in slab_mates:
        p_copy(b, sl).wait_send()
        bcast(b_buf, sl, b, me, b, b_s, b_r).wait_send()
    for t in mem_mates:
        bcast(om_all, me, t, t, sl, o_s, o_r).wait_send()
        bcast(x_all, me, t, t, sl, x_s, x_r).wait_send()
        for k in range(nch):
            fwd_copy(k, t // nc, t % nc, t, me).wait_send()
    for k in range(nch):
        for t in mem_mates:
            rev_copy(k, t, my_g, my_c, me).wait_send()
        for t in mem_mates:
            rev_copy(k, t, t // nc, t % nc, t).wait_recv()


def local(n_mem, n_slab, thickness, face_u, face_v, obs_cells, obs_weights, obs_values, obs_noise, cov_inverse,
          taper_mask):
    ml, rows, cols = thickness.shape
    ob = obs_values.shape[0]
    members = ml * n_mem
    nc, rc = split_blocks(rows, cols, n_mem)
    ng, cc = n_mem // nc, cols // nc
    ck = rc // 4 if rc % 4 == 0 else rc
    nch = rc // ck
    vmem = pl.BlockSpec(memory_space=pltpu.VMEM)
    hbm = pl.BlockSpec(memory_space=pl.ANY)
    dma = pltpu.SemaphoreType.DMA
    out = pl.pallas_call(
        functools.partial(kernel, n_mem, n_slab, nc, rc, ck),
        out_shape=jax.ShapeDtypeStruct((ng, nc, rc, ml, cc), F32),
        in_specs=[hbm] + [vmem] * 6 + [hbm, pl.BlockSpec(memory_space=pltpu.SMEM)],
        out_specs=hbm,
        scratch_shapes=[
            pltpu.VMEM((rows + 4, ml, cols), F32),
            pltpu.VMEM((rows + 8, cols), F32),
            pltpu.VMEM((3, ml, cols), F32),
            pltpu.VMEM((2, ml, cols), F32),
            pltpu.VMEM((3, ml, cols), F32),
            pltpu.VMEM((2, ml, cols), F32),
            pltpu.VMEM((ng, nc, rc, ml, cc), F32),
            pltpu.VMEM((n_mem, rc, ml, cc), F32),
            pltpu.VMEM((n_mem, rc, ml, cc), F32),
            pltpu.VMEM((rows * ml, 2 * ob), F32),
            pltpu.VMEM((rows, 2 * ob), F32),
            pltpu.VMEM((n_mem, ml, ob), F32),
            pltpu.VMEM((n_slab, ml, ob), F32),
            pltpu.VMEM((n_slab, ml, ob), F32),
            pltpu.VMEM((n_slab, ml, members), F32),
            pltpu.VMEM((n_mem, ml, members), F32),
            pltpu.VMEM((ml, rows, cols), F32),
            pltpu.VMEM((ob, n_slab * ob), F32),
            dma((2,)),
            dma((2,)), dma((2,)),
            dma((nch, n_mem)), dma((nch, n_mem)),
            dma((n_mem,)), dma((n_mem,)),
            dma((n_slab,)), dma((n_slab,)),
            dma((n_slab,)), dma((n_slab,)),
            dma((n_mem,)), dma((n_mem,)),
            dma((nch, n_mem)), dma((nch, n_mem)),
        ],
        compiler_params=pltpu.CompilerParams(collective_id=0, has_side_effects=True),
    )(
        thickness, face_u, face_v, obs_cells.T, obs_weights.T,
        obs_values.reshape(1, ob), obs_noise, cov_inverse, taper_mask,
    )
    return out.transpose(3, 0, 2, 1, 4).reshape(ml, rows, cols)


def solution(mesh):
    return jax.shard_map(
        functools.partial(local, mesh.shape["mem"], mesh.shape["slab"]),
        mesh=mesh,
        in_specs=(
            P("mem", "slab", None),
            P("slab", None),
            P("slab", None),
            P("slab", None),
            P("slab", None),
            P("slab"),
            P("mem", "slab"),
            P("slab", None),
            P(),
        ),
        out_specs=P("mem", "slab", None),
        check_vma=False,
    )
```
